256 devices in a mesh: ctx: 128 (over x_hi, y, z, core), head: 2 (over x_lo).
Axes of the slice: x: 4 (x_hi: 2, x_lo: 2; x = x_hi * 2 + x_lo), y: 4, z: 8, core: 2. Of those that a mesh axis runs over, the one named last changes fastest.
Arguments:
- queries: bfloat16 [32768, 2048], P(('ctx', 'head')), may hold values from -5 to 5
- keys: bfloat16 [32768, 2048], P(('ctx', 'head')), may hold values from -4 to 4
- values: bfloat16 [32768, 2048], P(('ctx', 'head')), may hold values from -6 to 6
- grad_out: bfloat16 [32768, 2048], P(('ctx', 'head')), may hold values from -6 to 6
- level_mask: int32 [256, 9], replicated, may hold values 0 or 1
Outputs:
- attended: bfloat16 [32768, 2048], P(('ctx', 'head'))
- grad_queries: bfloat16 [32768, 2048], P(('ctx', 'head'))
- grad_keys: bfloat16 [32768, 2048], P(('ctx', 'head'))
- grad_values: bfloat16 [32768, 2048], P(('ctx', 'head'))
The draws below stay inside these ranges and needn't reach their ends.
All inputs are finite; a program needn't handle non-finite values.
Results may differ from the reference program's by a relative error of at most 0.011.
Values may be sent and summed in bfloat16 or wider, within the bound.
A program may use at most 128 MiB of HBM per device.

```python
import jax
import jax.numpy as jnp
from jax import lax

HD = 128
HEADS = 16
BLK = 128
LEVELS = 9
NB = 256
SEQ = 32768


def draw_queries(key, part):
    drawn = jax.random.truncated_normal(jax.random.fold_in(key, 1), -4.0, 4.0, (SEQ, HEADS * HD))
    return drawn.astype(jnp.float32).astype(jnp.bfloat16)


def draw_keys(key, part):
    drawn = jax.random.truncated_normal(jax.random.fold_in(key, 5), -4.0, 4.0, (SEQ, HEADS * HD))
    return drawn.astype(jnp.float32).astype(jnp.bfloat16)


def set_ends(entries, stream_key, low, largest):
    place = [jax.random.randint(jax.random.fold_in(stream_key, axis), (), 0, length) for axis, length in enumerate(entries.shape)]
    widest = entries.shape.index(max(entries.shape))
    neighbour = place[:widest] + [(place[widest] + 1) % entries.shape[widest]] + place[widest + 1:]
    return entries.at[tuple(place)].set(low).at[tuple(neighbour)].set(largest)


def levels(key, dims, cuts, least, top_value):
    level, own = 1.0, jax.random.fold_in(key, 6)
    for dim, blocks in cuts:
        draws = jnp.exp(jax.random.uniform(jax.random.fold_in(own, dim), (blocks,), jnp.float32, least / len(cuts), top_value / len(cuts)))
        level = level * jnp.repeat(draws, dims[dim] // blocks).reshape([-1 if axis == dim else 1 for axis in range(len(dims))])
    return level


def gaussian(key, dims, scale, bound, shards=(), held_as=jnp.bfloat16):
    values = scale * jax.random.normal(key, dims, jnp.float32)
    if shards:
        values = values * levels(key, dims, shards, -0.22, 0.18)
    return jnp.clip(values, -bound, bound).astype(held_as)


def setup_inputs(seed: int = 0) -> dict:
    key_list = jax.random.split(jax.random.key(seed), 6)
    return {
        "queries": draw_queries(jax.random.fold_in(key_list[5], 71), 0),
        "keys": draw_keys(jax.random.fold_in(key_list[5], 71), 0),
        "values": gaussian(key_list[2], (SEQ, HEADS * HD), 1.0, 6.0, ((0, 256),)),
        "grad_out": gaussian(key_list[3], (SEQ, HEADS * HD), 1.0, 6.0, ((0, 256),)),
        "level_mask": set_ends((jax.random.randint(key_list[4], (NB, LEVELS), 0, 4) < 3).astype(jnp.int32), jax.random.fold_in(key_list[4], 1), 0, 1),
    }


masked_value = -1e30


def reference(queries, keys, values, grad_out, level_mask):
    seq_len = queries.shape[0]
    head_count = queries.shape[1] // HD
    blk_count = seq_len // BLK
    softmax_scale = HD ** -0.5
    shape4 = (blk_count, BLK, head_count, HD)
    q_blocks = queries.reshape(shape4)
    k_blocks = keys.reshape(shape4)
    v_blocks = values.reshape(shape4)
    g_blocks = grad_out.reshape(shape4)
    distances = (2 ** jnp.arange(LEVELS)).astype(jnp.int32)
    causal = jnp.tril(jnp.ones((BLK, BLK), dtype=bool))

    def query_side(block):
        key_ids = block - distances
        usable = (key_ids >= 0) & (level_mask[block] == 1)
        ids = jnp.concatenate([block[None], jnp.maximum(key_ids, 0)]).astype(jnp.int32)
        key_set = k_blocks[ids].reshape(-1, head_count, HD).astype(jnp.float32)
        value_set = v_blocks[ids].reshape(-1, head_count, HD).astype(jnp.float32)
        level_part = jnp.broadcast_to(jnp.repeat(usable, BLK)[None, :], (BLK, LEVELS * BLK))
        permit = jnp.concatenate([causal, level_part], 1)
        single_query_block = q_blocks[block].astype(jnp.float32)
        scores = jnp.einsum('qhd,khd->hqk', single_query_block, key_set) * softmax_scale
        scores = jnp.where(permit[None], scores, masked_value)
        top_score = jnp.max(scores, -1, keepdims=True)
        lse = top_score[..., 0] + jnp.log(jnp.sum(jnp.exp(scores - top_score), -1))
        probs = jnp.exp(scores - lse[..., None])
        rounded_result = probs.astype(jnp.bfloat16)
        attended = jnp.einsum('hqk,khd->qhd', rounded_result.astype(jnp.float32), value_set).astype(jnp.bfloat16)
        single_output_gradient = g_blocks[block].astype(jnp.float32)
        delta = jnp.sum(single_output_gradient * attended.astype(jnp.float32), -1).T
        probability_gradient = jnp.einsum('qhd,khd->hqk', single_output_gradient, value_set)
        score_gradient = (probs * (probability_gradient - delta[..., None])).astype(jnp.bfloat16)
        grad_q = (softmax_scale * jnp.einsum('hqk,khd->qhd', score_gradient.astype(jnp.float32), key_set)).astype(jnp.bfloat16)
        return attended, grad_q, lse, delta

    attended, grad_q, lse_all, delta_all = lax.map(query_side, jnp.arange(blk_count, dtype=jnp.int32))

    def key_side(block):
        query_ids = block + distances
        clipped = jnp.minimum(query_ids, blk_count - 1).astype(jnp.int32)
        usable = (query_ids < blk_count) & (level_mask[clipped, jnp.arange(LEVELS)] == 1)
        ids = jnp.concatenate([block[None], clipped]).astype(jnp.int32)
        query_set = q_blocks[ids].reshape(-1, head_count, HD).astype(jnp.float32)
        grad_set = g_blocks[ids].reshape(-1, head_count, HD).astype(jnp.float32)
        lse_set = lse_all[ids].transpose(1, 0, 2).reshape(head_count, -1)
        delta_set = delta_all[ids].transpose(1, 0, 2).reshape(head_count, -1)
        level_part = jnp.broadcast_to(jnp.repeat(usable, BLK)[:, None], (LEVELS * BLK, BLK))
        permit = jnp.concatenate([causal, level_part], 0)
        single_key_block = k_blocks[block].astype(jnp.float32)
        single_value_block = v_blocks[block].astype(jnp.float32)
        scores = jnp.einsum('qhd,khd->hqk', query_set, single_key_block) * softmax_scale
        scores = jnp.where(permit[None], scores, masked_value)
        probs = jnp.exp(scores - lse_set[..., None])
        rounded_result = probs.astype(jnp.bfloat16)
        probability_gradient = jnp.einsum('qhd,khd->hqk', grad_set, single_value_block)
        score_gradient = (probs * (probability_gradient - delta_set[..., None])).astype(jnp.bfloat16)
        grad_k = (softmax_scale * jnp.einsum('hqk,qhd->khd', score_gradient.astype(jnp.float32), query_set)).astype(jnp.bfloat16)
        grad_v = jnp.einsum('hqk,qhd->khd', rounded_result.astype(jnp.float32), grad_set).astype(jnp.bfloat16)
        return grad_k, grad_v

    grad_k, grad_v = lax.map(key_side, jnp.arange(blk_count, dtype=jnp.int32))
    flat = (seq_len, head_count * HD)
    return attended.reshape(flat), grad_q.reshape(flat), grad_k.reshape(flat), grad_v.reshape(flat)
```

```python
import jax
import jax.numpy as jnp
from jax import lax
from jax.experimental import pallas as pl
from jax.experimental.pallas import tpu as pltpu
from jax.sharding import PartitionSpec as P

HD = 128
BLK = 128
LEVELS = 9
NB = 256
H = 16
FAR = 8
OWN = FAR
SLOTS = FAR + 1
WIDE = SLOTS * BLK
NEG = -1e30
SCALE = HD ** (-0.5)
LOG2E = 1.4426950408889634
MESH = pl.DeviceIdType.MESH

RELAY1 = 2
RELAY2 = 4
QUERY = 6
KEY = 7


def dot_nt(a, b):
    return lax.dot_general(a, b, (((1,), (1,)), ((), ())), preferred_element_type=jnp.float32)


def dot_nn(a, b):
    return lax.dot_general(a, b, (((1,), (0,)), ((), ())), preferred_element_type=jnp.float32)


def place(block):
    return (block // 2, block % 2)


def kernel(
    q_hbm, k_hbm, v_hbm, g_hbm, lm_ref,
    o_hbm, dq_hbm, dk_hbm, dv_hbm,
    kv, qg, st, p_s, pb, dsb, ob, bias,
    load_sem, send_sem, recv_sem, st_send, st_recv, out_sem,
):
    me = lax.axis_index("ctx") * 2 + lax.axis_index("head")
    bufs = (kv, qg)
    index = (me, NB - 1 - me)

    def real(side, m):
        return m if side == 0 else NB - 1 - m

    def copy(side, src, level, head, target):
        buf = bufs[side]
        return pltpu.make_async_remote_copy(
            src_ref=buf.at[head, :, src],
            dst_ref=buf.at[head, :, level],
            send_sem=send_sem.at[side, level],
            recv_sem=recv_sem.at[side, level, head],
            device_id=place(real(side, target)),
            device_id_type=MESH,
        )

    def send(side, src, level, head, target, cond):
        @pl.when(cond)
        def _():
            copy(side, src, level, head, target).start()

    def wait_recv(side, level, head):
        @pl.when(index[side] >= 2**level)
        def _():
            copy(side, OWN, level, head, index[side]).wait_recv()

    def loads(head):
        cols = pl.ds(pl.multiple_of(head * HD, HD), HD)
        return [
            pltpu.make_async_copy(k_hbm.at[:, cols], kv.at[head, 0, OWN], load_sem.at[0, head]),
            pltpu.make_async_copy(v_hbm.at[:, cols], kv.at[head, 1, OWN], load_sem.at[1, head]),
            pltpu.make_async_copy(q_hbm.at[:, cols], qg.at[head, 0, OWN], load_sem.at[2, head]),
            pltpu.make_async_copy(g_hbm.at[:, cols], qg.at[head, 1, OWN], load_sem.at[3, head]),
        ]

    @pl.loop(0, H)
    def _(head):
        for c in loads(head):
            c.start()

    for side in range(2):
        for level in range(FAR):

            @pl.when(index[side] < 2**level)
            def _(side=side, level=level):
                @pl.loop(0, H)
                def _(head):
                    bufs[side][head, :, level] = jnp.zeros((2, BLK, HD), jnp.bfloat16)
                    if side == 1:
                        st[head, level] = jnp.zeros((8, BLK), jnp.float32)

    for level in range(FAR):
        d = 2**level
        bias[0, level] = jnp.where((lm_ref[me, level] == 1) & (me >= d), 0.0, NEG)
        later = jnp.minimum(me + d, NB - 1)
        bias[1, level] = jnp.where((lm_ref[later, level] == 1) & (me + d < NB), 0.0, NEG)

    barrier = pltpu.get_barrier_semaphore()
    count = jnp.where((me % 4 == 0) | (me % 4 == 3), 1, 0)
    for level in range(FAR):
        d = 2**level
        count = count + jnp.where(me >= d, 1, 0) + jnp.where(me + d < NB, 1, 0)

        @pl.when(me >= d)
        def _(d=d):
            pl.semaphore_signal(barrier, inc=1, device_id=place(me - d), device_id_type=MESH)

        @pl.when(me + d < NB)
        def _(d=d):
            pl.semaphore_signal(barrier, inc=1, device_id=place(me + d), device_id_type=MESH)

    @pl.when(me % 4 == 0)
    def _():
        pl.semaphore_signal(barrier, inc=1, device_id=place(me + 3), device_id_type=MESH)

    @pl.when(me % 4 == 3)
    def _():
        pl.semaphore_signal(barrier, inc=1, device_id=place(me - 3), device_id_type=MESH)

    pl.semaphore_wait(barrier, count)

    def sends_own(side):
        m = index[side]
        return [
            (2, m + 4, m + 4 < NB),
            (5, m + 32, m + 32 < NB),
            (7, m + 128, m + 128 < NB),
            (0, m + 1, m % 4 != 3),
            (1, m + 2, m % 4 < 2),
        ]

    def sends_near(side):
        m = index[side]
        return [
            (3, m + 4, (m >= 4) & (m + 4 < NB)),
            (0, m - 3, (m >= 4) & (m % 4 == 3)),
            (1, m - 2, (m >= 4) & (m % 4 >= 2)),
        ]

    def sends_mid(side):
        m = index[side]
        return [(6, m + 32, (m >= 32) & (m + 32 < NB))]

    def sends_far(side):
        m = index[side]
        return [(4, m + 8, (m >= 8) & (m + 8 < NB))]

    def own(head):
        for c in loads(head):
            c.wait()
        for i in range(5):
            for side in range(2):
                level, target, cond = sends_own(side)[i]
                send(side, OWN, level, head, target, cond)

    def relay1(head):
        for side in range(2):
            wait_recv(side, 2, head)
            for level, target, cond in sends_near(side):
                send(side, 2, level, head, target, cond)
        for side in range(2):
            wait_recv(side, 5, head)
            for level, target, cond in sends_mid(side):
                send(side, 5, level, head, target, cond)

    def relay2(head):
        for side in range(2):
            wait_recv(side, 3, head)
            for level, target, cond in sends_far(side):
                send(side, 3, level, head, target, cond)

    def stat_copy(level, head):
        return pltpu.make_async_remote_copy(
            src_ref=st.at[head, OWN],
            dst_ref=st.at[head, level],
            send_sem=st_send.at[level],
            recv_sem=st_recv.at[level, head],
            device_id=place(me - 2**level),
            device_id_type=MESH,
        )

    def stores(head, which):
        cols = pl.ds(pl.multiple_of(head * HD, HD), HD)
        return [
            pltpu.make_async_copy(ob.at[i, head], (o_hbm, dq_hbm, dk_hbm, dv_hbm)[i].at[:, cols], out_sem.at[i, head])
            for i in which
        ]

    row_id = lax.broadcasted_iota(jnp.int32, (BLK, BLK), 0)
    col_id = lax.broadcasted_iota(jnp.int32, (BLK, BLK), 1)

    def span(slot):
        return pl.ds(slot * BLK, BLK)

    def query_side(head):
        for level in (0, 1, 7, 6, 4):
            wait_recv(0, level, head)
        q = qg[head, 0, OWN]
        g = qg[head, 1, OWN]
        top = None
        for slot in range(SLOTS):
            s = dot_nt(q, kv[head, 0, slot]) * (SCALE * LOG2E)
            s = jnp.where(row_id >= col_id, s, NEG) if slot == OWN else s + bias[0, slot]
            p_s[:, span(slot)] = s
            top = s if top is None else jnp.maximum(top, s)
        top = jnp.max(top, axis=1, keepdims=True)
        total = None
        for slot in range(SLOTS):
            p = jnp.exp2(p_s[:, span(slot)] - top)
            p_s[:, span(slot)] = p
            pb[:, span(slot)] = p.astype(jnp.bfloat16)
            total = p if total is None else total + p
        total = jnp.sum(total, axis=1, keepdims=True)
        inverse = 1.0 / total
        o = dot_nn(pb[...], kv[head, 1].reshape(WIDE, HD)) * inverse
        o = o.astype(jnp.bfloat16)
        ob[0, head] = o
        delta = jnp.sum(g.astype(jnp.float32) * o.astype(jnp.float32), axis=1, keepdims=True)
        lse = top + jnp.log2(total)
        st[head, OWN] = jnp.where(col_id == 0, lse, delta).T[:8]
        for level in range(FAR):

            @pl.when(me >= 2**level)
            def _(level=level):
                stat_copy(level, head).start()

        for slot in range(SLOTS):
            dp = dot_nt(g, kv[head, 1, slot])
            dsb[:, span(slot)] = (p_s[:, span(slot)] * (dp - delta)).astype(jnp.bfloat16)
        dq = dot_nn(dsb[...], kv[head, 0].reshape(WIDE, HD)) * (inverse * SCALE)
        ob[1, head] = dq.astype(jnp.bfloat16)
        for c in stores(head, (0, 1)):
            c.start()

    def key_side(head):
        for level in (0, 1, 7, 6, 4):
            wait_recv(1, level, head)
        for level in range(FAR):

            @pl.when(me + 2**level < NB)
            def _(level=level):
                stat_copy(level, head).wait_recv()

        k = kv[head, 0, OWN]
        v = kv[head, 1, OWN]
        for slot in range(SLOTS):
            s = dot_nt(k, qg[head, 0, slot]) * (SCALE * LOG2E) - st[head, slot, 0:1, :]
            s = jnp.where(row_id <= col_id, s, NEG) if slot == OWN else s + bias[1, slot]
            p = jnp.exp2(s)
            pb[:, span(slot)] = p.astype(jnp.bfloat16)
            dp = dot_nt(v, qg[head, 1, slot])
            dsb[:, span(slot)] = (p * (dp - st[head, slot, 1:2, :])).astype(jnp.bfloat16)
        ob[3, head] = dot_nn(pb[...], qg[head, 1].reshape(WIDE, HD)).astype(jnp.bfloat16)
        ob[2, head] = (dot_nn(dsb[...], qg[head, 0].reshape(WIDE, HD)) * SCALE).astype(jnp.bfloat16)
        for c in stores(head, (2, 3)):
            c.start()

    @pl.loop(0, H + KEY)
    def _(step):
        for stage, lag in ((own, 0), (relay1, RELAY1), (relay2, RELAY2), (query_side, QUERY), (key_side, KEY)):

            @pl.when((step >= lag) & (step < H + lag))
            def _(stage=stage, lag=lag):
                stage(step - lag)

    for side in range(2):
        m = index[side]
        sent = {0: (m % 4 != 3) | (m >= 4), 1: (m % 4 < 2) | (m >= 4)}
        for level, target, cond in [s for group in (sends_own, sends_near, sends_mid, sends_far) for s in group(side)]:
            if level in (0, 1):
                if level not in sent:
                    continue
                cond = sent.pop(level)

            @pl.when(cond)
            def _(side=side, level=level, target=target):
                pltpu.make_async_remote_copy(
                    src_ref=bufs[side].at[:, :, OWN],
                    dst_ref=bufs[side].at[:, :, level],
                    send_sem=send_sem.at[side, level],
                    recv_sem=recv_sem.at[side, level, 0],
                    device_id=place(real(side, target)),
                    device_id_type=MESH,
                ).wait_send()

    for level in range(FAR):

        @pl.when(me >= 2**level)
        def _(level=level):
            pltpu.make_async_remote_copy(
                src_ref=st.at[:, OWN],
                dst_ref=st.at[:, level],
                send_sem=st_send.at[level],
                recv_sem=st_recv.at[level, 0],
                device_id=place(me - 2**level),
                device_id_type=MESH,
            ).wait_send()

    @pl.loop(0, H)
    def _(head):
        for c in stores(head, range(4)):
            c.wait()


def local(queries, keys, values, grad_out, level_mask):
    any_space = pl.BlockSpec(memory_space=pl.ANY)
    out = jax.ShapeDtypeStruct((BLK, H * HD), jnp.bfloat16)
    return tuple(
        pl.pallas_call(
            kernel,
            name="log_sparse",
            out_shape=(out, out, out, out),
            in_specs=[any_space] * 4 + [pl.BlockSpec(memory_space=pltpu.SMEM)],
            out_specs=(any_space,) * 4,
            scratch_shapes=[
                pltpu.VMEM((H, 2, SLOTS, BLK, HD), jnp.bfloat16),
                pltpu.VMEM((H, 2, SLOTS, BLK, HD), jnp.bfloat16),
                pltpu.VMEM((H, SLOTS, 8, BLK), jnp.float32),
                pltpu.VMEM((BLK, WIDE), jnp.float32),
                pltpu.VMEM((BLK, WIDE), jnp.bfloat16),
                pltpu.VMEM((BLK, WIDE), jnp.bfloat16),
                pltpu.VMEM((4, H, BLK, HD), jnp.bfloat16),
                pltpu.SMEM((2, FAR), jnp.float32),
                pltpu.SemaphoreType.DMA((4, H)),
                pltpu.SemaphoreType.DMA((2, FAR)),
                pltpu.SemaphoreType.DMA((2, FAR, H)),
                pltpu.SemaphoreType.DMA((FAR,)),
                pltpu.SemaphoreType.DMA((FAR, H)),
                pltpu.SemaphoreType.DMA((4, H)),
            ],
            compiler_params=pltpu.CompilerParams(
                collective_id=0, has_side_effects=True, vmem_limit_bytes=48 << 20
            ),
        )(queries, keys, values, grad_out, level_mask)
    )


def solution(mesh):
    rows = P(("ctx", "head"), None)
    return jax.shard_map(
        local,
        mesh=mesh,
        in_specs=(rows, rows, rows, rows, P()),
        out_specs=(rows, rows, rows, rows),
        check_vma=False,
    )
```

```python
import jax
import jax.numpy as jnp
from jax import lax
from jax.experimental import pallas as pl
from jax.experimental.pallas import tpu as pltpu
from jax.sharding import PartitionSpec as P

HD = 128
BLK = 128
LEVELS = 9
NB = 256
H = 16
FAR = 8
OWN = FAR
SLOTS = FAR + 1
SECOND = FAR
WIDE = SLOTS * BLK
NEG = -1e30
SCALE = HD ** (-0.5)
LOG2E = 1.4426950408889634
MESH = pl.DeviceIdType.MESH

ROW = 1
BACK = 2
NEAR = 3
FARTHER = 5
QUERY = 7
KEY = 8


def dot_nt(a, b):
    return lax.dot_general(a, b, (((1,), (1,)), ((), ())), preferred_element_type=jnp.float32)


def dot_nn(a, b):
    return lax.dot_general(a, b, (((1,), (0,)), ((), ())), preferred_element_type=jnp.float32)


def place(block):
    return (block // 2, block % 2)


def kernel(
    q_hbm, k_hbm, v_hbm, g_hbm, lm_ref,
    o_hbm, dq_hbm, dk_hbm, dv_hbm,
    kv, qg, st, p_s, pb, dsb, ob, bias,
    load_sem, send_sem, recv_sem, st_send, st_recv, out_sem,
):
    me = lax.axis_index("ctx") * 2 + lax.axis_index("head")
    bufs = (kv, qg)
    index = (me, NB - 1 - me)

    def real(side, m):
        return m if side == 0 else NB - 1 - m

    def copy(side, src, level, head, target):
        buf = bufs[side]
        slot = level
        level = 6 if level == SECOND else level
        return pltpu.make_async_remote_copy(
            src_ref=buf.at[head, :, src],
            dst_ref=buf.at[head, :, level],
            send_sem=send_sem.at[side, slot],
            recv_sem=recv_sem.at[side, level, head],
            device_id=place(real(side, target)),
            device_id_type=MESH,
        )

    def send(side, src, level, head, target, cond):
        @pl.when(cond)
        def _():
            copy(side, src, level, head, target).start()

    def wait_recv(side, level, head):
        @pl.when(index[side] >= 2**level)
        def _():
            copy(side, OWN, level, head, index[side]).wait_recv()

    def loads(head):
        cols = pl.ds(pl.multiple_of(head * HD, HD), HD)
        return [
            pltpu.make_async_copy(k_hbm.at[:, cols], kv.at[head, 0, OWN], load_sem.at[0, head]),
            pltpu.make_async_copy(v_hbm.at[:, cols], kv.at[head, 1, OWN], load_sem.at[1, head]),
            pltpu.make_async_copy(q_hbm.at[:, cols], qg.at[head, 0, OWN], load_sem.at[2, head]),
            pltpu.make_async_copy(g_hbm.at[:, cols], qg.at[head, 1, OWN], load_sem.at[3, head]),
        ]

    @pl.loop(0, H)
    def _(head):
        for c in loads(head):
            c.start()

    for side in range(2):
        for level in range(FAR):

            @pl.when(index[side] < 2**level)
            def _(side=side, level=level):
                @pl.loop(0, H)
                def _(head):
                    bufs[side][head, :, level] = jnp.zeros((2, BLK, HD), jnp.bfloat16)
                    if side == 1:
                        st[head, level] = jnp.zeros((8, BLK), jnp.float32)

    for level in range(FAR):
        d = 2**level
        bias[0, level] = jnp.where((lm_ref[me, level] == 1) & (me >= d), 0.0, NEG)
        later = jnp.minimum(me + d, NB - 1)
        bias[1, level] = jnp.where((lm_ref[later, level] == 1) & (me + d < NB), 0.0, NEG)

    barrier = pltpu.get_barrier_semaphore()
    part, line, row = me % 4, (me // 4) % 8, me // 32
    partners = [(3, part == 0), (-3, part == 3), (28, line == 0), (-28, line == 7)]
    partners += [(96, row == 4), (-96, row == 7), (96, row == 0), (-96, row == 3)]
    for level in range(FAR):
        d = 2**level
        partners += [(-d, me >= d), (d, me + d < NB)]
    count = 0
    for d, cond in partners:
        count = count + jnp.where(cond, 1, 0)

        @pl.when(cond)
        def _(d=d):
            pl.semaphore_signal(barrier, inc=1, device_id=place(me + d), device_id_type=MESH)

    pl.semaphore_wait(barrier, count)

    def sends_own(m):
        line, row = (m // 4) % 8, m // 32
        return [
            (2, m + 4, line < 7),
            (7, m + 128, row < 4),
            (5, m + 32, (row != 3) & (row < 7)),
            (0, m + 1, m % 4 != 3),
            (1, m + 2, m % 4 < 2),
        ]

    def sends_7(m):
        row = m // 32
        return [(5, m - 96, row == 7), (6, m - 64, row == 6)]

    def sends_5(m):
        line, row = (m // 4) % 8, m // 32
        return [(2, m - 28, (line == 7) & (row >= 1)), (SECOND, m + 32, (row >= 1) & (row < 7) & (row != 3))]

    def sends_2(m):
        return [
            (3, m + 4, (m >= 4) & (m + 4 < NB)),
            (0, m - 3, (m >= 4) & (m % 4 == 3)),
            (1, m - 2, (m >= 4) & (m % 4 >= 2)),
        ]

    def sends_3(m):
        return [(4, m + 8, (m >= 8) & (m + 8 < NB))]

    def own(head):
        for c in loads(head):
            c.wait()
        for i in range(5):
            for side in range(2):
                level, target, cond = sends_own(index[side])[i]
                send(side, OWN, level, head, target, cond)

    def relay(slot, sends):
        def stage(head):
            for side in range(2):
                wait_recv(side, slot, head)
                for level, target, cond in sends(index[side]):
                    send(side, slot, level, head, target, cond)

        return stage

    def stat_copy(level, head):
        return pltpu.make_async_remote_copy(
            src_ref=st.at[head, OWN],
            dst_ref=st.at[head, level],
            send_sem=st_send.at[level],
            recv_sem=st_recv.at[level, head],
            device_id=place(me - 2**level),
            device_id_type=MESH,
        )

    def stores(head, which):
        cols = pl.ds(pl.multiple_of(head * HD, HD), HD)
        return [
            pltpu.make_async_copy(ob.at[i, head], (o_hbm, dq_hbm, dk_hbm, dv_hbm)[i].at[:, cols], out_sem.at[i, head])
            for i in which
        ]

    row_id = lax.broadcasted_iota(jnp.int32, (BLK, BLK), 0)
    col_id = lax.broadcasted_iota(jnp.int32, (BLK, BLK), 1)

    def span(slot):
        return pl.ds(slot * BLK, BLK)

    def query_side(head):
        for level in (0, 1, 6, 4):
            wait_recv(0, level, head)
        q = qg[head, 0, OWN]
        g = qg[head, 1, OWN]
        top = None
        for slot in range(SLOTS):
            s = dot_nt(q, kv[head, 0, slot]) * (SCALE * LOG2E)
            s = jnp.where(row_id >= col_id, s, NEG) if slot == OWN else s + bias[0, slot]
            p_s[:, span(slot)] = s
            top = s if top is None else jnp.maximum(top, s)
        top = jnp.max(top, axis=1, keepdims=True)
        total = None
        for slot in range(SLOTS):
            p = jnp.exp2(p_s[:, span(slot)] - top)
            p_s[:, span(slot)] = p
            pb[:, span(slot)] = p.astype(jnp.bfloat16)
            total = p if total is None else total + p
        total = jnp.sum(total, axis=1, keepdims=True)
        inverse = 1.0 / total
        o = dot_nn(pb[...], kv[head, 1].reshape(WIDE, HD)) * inverse
        o = o.astype(jnp.bfloat16)
        ob[0, head] = o
        delta = jnp.sum(g.astype(jnp.float32) * o.astype(jnp.float32), axis=1, keepdims=True)
        lse = top + jnp.log2(total)
        st[head, OWN] = jnp.where(col_id == 0, lse, delta).T[:8]
        for level in range(FAR):

            @pl.when(me >= 2**level)
            def _(level=level):
                stat_copy(level, head).start()

        for slot in range(SLOTS):
            dp = dot_nt(g, kv[head, 1, slot])
            dsb[:, span(slot)] = (p_s[:, span(slot)] * (dp - delta)).astype(jnp.bfloat16)
        dq = dot_nn(dsb[...], kv[head, 0].reshape(WIDE, HD)) * (inverse * SCALE)
        ob[1, head] = dq.astype(jnp.bfloat16)
        for c in stores(head, (0, 1)):
            c.start()

    def key_side(head):
        for level in (0, 1, 6, 4):
            wait_recv(1, level, head)
        for level in range(FAR):

            @pl.when(me + 2**level < NB)
            def _(level=level):
                stat_copy(level, head).wait_recv()

        k = kv[head, 0, OWN]
        v = kv[head, 1, OWN]
        for slot in range(SLOTS):
            s = dot_nt(k, qg[head, 0, slot]) * (SCALE * LOG2E) - st[head, slot, 0:1, :]
            s = jnp.where(row_id <= col_id, s, NEG) if slot == OWN else s + bias[1, slot]
            p = jnp.exp2(s)
            pb[:, span(slot)] = p.astype(jnp.bfloat16)
            dp = dot_nt(v, qg[head, 1, slot])
            dsb[:, span(slot)] = (p * (dp - st[head, slot, 1:2, :])).astype(jnp.bfloat16)
        ob[3, head] = dot_nn(pb[...], qg[head, 1].reshape(WIDE, HD)).astype(jnp.bfloat16)
        ob[2, head] = (dot_nn(dsb[...], qg[head, 0].reshape(WIDE, HD)) * SCALE).astype(jnp.bfloat16)
        for c in stores(head, (2, 3)):
            c.start()

    @pl.loop(0, H + KEY)
    def _(step):
        for stage, lag in (
            (own, 0),
            (relay(7, sends_7), ROW),
            (relay(5, sends_5), BACK),
            (relay(2, sends_2), NEAR),
            (relay(3, sends_3), FARTHER),
            (query_side, QUERY),
            (key_side, KEY),
        ):

            @pl.when((step >= lag) & (step < H + lag))
            def _(stage=stage, lag=lag):
                stage(step - lag)

    for side in range(2):
        m = index[side]
        line, row = (m // 4) % 8, m // 32
        conds = (
            (m % 4 != 3) | (m >= 4),
            (m % 4 < 2) | (m >= 4),
            (line < 7) | (row >= 1),
            (m >= 4) & (m + 4 < NB),
            (m >= 8) & (m + 8 < NB),
            row != 3,
            row == 6,
            row < 4,
            (row >= 1) & (row < 7) & (row != 3),
        )
        for slot, cond in enumerate(conds):

            @pl.when(cond)
            def _(side=side, slot=slot):
                pltpu.make_async_remote_copy(
                    src_ref=bufs[side].at[:, :, OWN],
                    dst_ref=bufs[side].at[:, :, 0],
                    send_sem=send_sem.at[side, slot],
                    recv_sem=recv_sem.at[side, 0, 0],
                    device_id=place(me),
                    device_id_type=MESH,
                ).wait_send()

    for level in range(FAR):

        @pl.when(me >= 2**level)
        def _(level=level):
            pltpu.make_async_remote_copy(
                src_ref=st.at[:, OWN],
                dst_ref=st.at[:, level],
                send_sem=st_send.at[level],
                recv_sem=st_recv.at[level, 0],
                device_id=place(me - 2**level),
                device_id_type=MESH,
            ).wait_send()

    @pl.loop(0, H)
    def _(head):
        for c in stores(head, range(4)):
            c.wait()


def local(queries, keys, values, grad_out, level_mask):
    any_space = pl.BlockSpec(memory_space=pl.ANY)
    out = jax.ShapeDtypeStruct((BLK, H * HD), jnp.bfloat16)
    return tuple(
        pl.pallas_call(
            kernel,
            name="log_sparse",
            out_shape=(out, out, out, out),
            in_specs=[any_space] * 4 + [pl.BlockSpec(memory_space=pltpu.SMEM)],
            out_specs=(any_space,) * 4,
            scratch_shapes=[
                pltpu.VMEM((H, 2, SLOTS, BLK, HD), jnp.bfloat16),
                pltpu.VMEM((H, 2, SLOTS, BLK, HD), jnp.bfloat16),
                pltpu.VMEM((H, SLOTS, 8, BLK), jnp.float32),
                pltpu.VMEM((BLK, WIDE), jnp.float32),
                pltpu.VMEM((BLK, WIDE), jnp.bfloat16),
                pltpu.VMEM((BLK, WIDE), jnp.bfloat16),
                pltpu.VMEM((4, H, BLK, HD), jnp.bfloat16),
                pltpu.SMEM((2, FAR), jnp.float32),
                pltpu.SemaphoreType.DMA((4, H)),
                pltpu.SemaphoreType.DMA((2, FAR + 1)),
                pltpu.SemaphoreType.DMA((2, FAR, H)),
                pltpu.SemaphoreType.DMA((FAR,)),
                pltpu.SemaphoreType.DMA((FAR, H)),
                pltpu.SemaphoreType.DMA((4, H)),
            ],
            compiler_params=pltpu.CompilerParams(
                collective_id=0, has_side_effects=True, vmem_limit_bytes=48 << 20
            ),
        )(queries, keys, values, grad_out, level_mask)
    )


def solution(mesh):
    rows = P(("ctx", "head"), None)
    return jax.shard_map(
        local,
        mesh=mesh,
        in_specs=(rows, rows, rows, rows, P()),
        out_specs=(rows, rows, rows, rows),
        check_vma=False,
    )
```

```python
import jax
import jax.numpy as jnp
from jax import lax
from jax.experimental import pallas as pl
from jax.experimental.pallas import tpu as pltpu
from jax.sharding import PartitionSpec as P

HD = 128
BLK = 128
LEVELS = 9
NB = 256
H = 16
FAR = 8
OWN = FAR
SLOTS = FAR + 1
SECOND = FAR
WIDE = SLOTS * BLK
NEG = -1e30
SCALE = HD ** (-0.5)
LOG2E = 1.4426950408889634
MESH = pl.DeviceIdType.MESH

ROW = 1
BACK = 2
NEAR = 3
FARTHER = 4
QUERY = 5
KEY = 8


def dot_nt(a, b):
    return lax.dot_general(a, b, (((1,), (1,)), ((), ())), preferred_element_type=jnp.float32)


def dot_nn(a, b):
    return lax.dot_general(a, b, (((1,), (0,)), ((), ())), preferred_element_type=jnp.float32)


def place(block):
    return (block // 2, block % 2)


def kernel(
    q_hbm, k_hbm, v_hbm, g_hbm, lm_ref,
    o_hbm, dq_hbm, dk_hbm, dv_hbm,
    kv, qg, st, p_s, pb, dsb, pk, dsk, ob, bias,
    load_sem, send_sem, recv_sem, st_send, st_recv, out_sem,
):
    me = lax.axis_index("ctx") * 2 + lax.axis_index("head")
    bufs = (kv, qg)
    index = (me, NB - 1 - me)

    def real(side, m):
        return m if side == 0 else NB - 1 - m

    def copy(side, src, level, head, target):
        buf = bufs[side]
        slot = level
        level = 6 if level == SECOND else level
        return pltpu.make_async_remote_copy(
            src_ref=buf.at[head, :, src],
            dst_ref=buf.at[head, :, level],
            send_sem=send_sem.at[side, slot],
            recv_sem=recv_sem.at[side, level, head],
            device_id=place(real(side, target)),
            device_id_type=MESH,
        )

    def send(side, src, level, head, target, cond):
        @pl.when(cond)
        def _():
            copy(side, src, level, head, target).start()

    def wait_recv(side, level, head):
        @pl.when(index[side] >= 2**level)
        def _():
            copy(side, OWN, level, head, index[side]).wait_recv()

    def loads(head):
        cols = pl.ds(pl.multiple_of(head * HD, HD), HD)
        return [
            pltpu.make_async_copy(k_hbm.at[:, cols], kv.at[head, 0, OWN], load_sem.at[0, head]),
            pltpu.make_async_copy(v_hbm.at[:, cols], kv.at[head, 1, OWN], load_sem.at[1, head]),
            pltpu.make_async_copy(q_hbm.at[:, cols], qg.at[head, 0, OWN], load_sem.at[2, head]),
            pltpu.make_async_copy(g_hbm.at[:, cols], qg.at[head, 1, OWN], load_sem.at[3, head]),
        ]

    @pl.loop(0, H)
    def _(head):
        for c in loads(head):
            c.start()

    for level in range(FAR):
        d = 2**level
        bias[0, level] = jnp.where((lm_ref[me, level] == 1) & (me >= d), 0.0, NEG)
        later = jnp.minimum(me + d, NB - 1)
        bias[1, level] = jnp.where((lm_ref[later, level] == 1) & (me + d < NB), 0.0, NEG)

    barrier = pltpu.get_barrier_semaphore()
    part, line, row = me % 4, (me // 4) % 8, me // 32
    partners = [(3, part == 0), (-3, part == 3), (28, line == 0), (-28, line == 7)]
    partners += [(96, row == 4), (-96, row == 7), (96, row == 0), (-96, row == 3)]
    for level in range(FAR):
        d = 2**level
        partners += [(-d, me >= d), (d, me + d < NB)]
    count = 0
    for d, cond in partners:
        count = count + jnp.where(cond, 1, 0)

        @pl.when(cond)
        def _(d=d):
            pl.semaphore_signal(barrier, inc=1, device_id=place(me + d), device_id_type=MESH)

    pl.semaphore_wait(barrier, count)

    def sends_own(m):
        line, row = (m // 4) % 8, m // 32
        return [
            (2, m + 4, line < 7),
            (7, m + 128, row < 4),
            (5, m + 32, (row != 3) & (row < 7)),
            (0, m + 1, m % 4 != 3),
            (1, m + 2, m % 4 < 2),
        ]

    def sends_7(m):
        row = m // 32
        return [(5, m - 96, row == 7), (6, m - 64, row == 6)]

    def sends_5(m):
        line, row = (m // 4) % 8, m // 32
        return [(2, m - 28, (line == 7) & (row >= 1)), (SECOND, m + 32, (row >= 1) & (row < 7) & (row != 3))]

    def sends_2(m):
        return [
            (3, m + 4, (m >= 4) & (m + 4 < NB)),
            (0, m - 3, (m >= 4) & (m % 4 == 3)),
            (1, m - 2, (m >= 4) & (m % 4 >= 2)),
        ]

    def sends_3(m):
        return [(4, m + 8, (m >= 8) & (m + 8 < NB))]

    def own(head):
        for c in loads(head):
            c.wait()
        send_own(head)
        for side in range(2):
            for level in range(FAR):

                @pl.when(index[side] < 2**level)
                def _(side=side, level=level):
                    bufs[side][head, :, level] = jnp.zeros((2, BLK, HD), jnp.bfloat16)
                    if side == 1:
                        st[head, level] = jnp.zeros((8, BLK), jnp.float32)

    def send_own(head):
        for i in range(5):
            for side in range(2):
                level, target, cond = sends_own(index[side])[i]
                send(side, OWN, level, head, target, cond)

    def relay(slot, sends):
        def stage(head):
            for side in range(2):
                wait_recv(side, slot, head)
                for level, target, cond in sends(index[side]):
                    send(side, slot, level, head, target, cond)

        return stage

    def stat_copy(level, head):
        return pltpu.make_async_remote_copy(
            src_ref=st.at[head, OWN],
            dst_ref=st.at[head, level],
            send_sem=st_send.at[level],
            recv_sem=st_recv.at[level, head],
            device_id=place(me - 2**level),
            device_id_type=MESH,
        )

    def stores(head, which):
        cols = pl.ds(pl.multiple_of(head * HD, HD), HD)
        return [
            pltpu.make_async_copy(ob.at[i, head], (o_hbm, dq_hbm, dk_hbm, dv_hbm)[i].at[:, cols], out_sem.at[i, head])
            for i in which
        ]

    row_id = lax.broadcasted_iota(jnp.int32, (BLK, BLK), 0)
    col_id = lax.broadcasted_iota(jnp.int32, (BLK, BLK), 1)

    def span(slot):
        return pl.ds(slot * BLK, BLK)

    def query_waits(head):
        for level in (0, 1, 6, 4):
            wait_recv(0, level, head)

    def key_waits(head):
        for level in (0, 1, 6, 4):
            wait_recv(1, level, head)
        for level in range(FAR):

            @pl.when(me + 2**level < NB)
            def _(level=level):
                stat_copy(level, head).wait_recv()

    def query_parts(head):
        q = qg[head, 0, OWN]
        g = qg[head, 1, OWN]
        top = None
        for slot in range(SLOTS):
            s = dot_nt(q, kv[head, 0, slot]) * (SCALE * LOG2E)
            s = jnp.where(row_id >= col_id, s, NEG) if slot == OWN else s + bias[0, slot]
            p_s[:, span(slot)] = s
            top = s if top is None else jnp.maximum(top, s)
            yield
        top = jnp.max(top, axis=1, keepdims=True)
        yield
        total = None
        for slot in range(SLOTS):
            p = jnp.exp2(p_s[:, span(slot)] - top)
            p_s[:, span(slot)] = p
            pb[:, span(slot)] = p.astype(jnp.bfloat16)
            total = p if total is None else total + p
            yield
        total = jnp.sum(total, axis=1, keepdims=True)
        inverse = 1.0 / total
        o = dot_nn(pb[...], kv[head, 1].reshape(WIDE, HD)) * inverse
        o = o.astype(jnp.bfloat16)
        ob[0, head] = o
        delta = jnp.sum(g.astype(jnp.float32) * o.astype(jnp.float32), axis=1, keepdims=True)
        lse = top + jnp.log2(total)
        yield
        for slot in range(SLOTS):
            dp = dot_nt(g, kv[head, 1, slot])
            dsb[:, span(slot)] = (p_s[:, span(slot)] * (dp - delta)).astype(jnp.bfloat16)
            yield
        dq = dot_nn(dsb[...], kv[head, 0].reshape(WIDE, HD)) * (inverse * SCALE)
        ob[1, head] = dq.astype(jnp.bfloat16)
        st[head, OWN] = jnp.where(col_id == 0, lse, delta).T[:8]

    def query_done(head):
        for level in range(FAR):

            @pl.when(me >= 2**level)
            def _(level=level):
                stat_copy(level, head).start()

        for c in stores(head, (0, 1)):
            c.start()

    def key_parts(head):
        k = kv[head, 0, OWN]
        v = kv[head, 1, OWN]
        for slot in range(SLOTS):
            s = dot_nt(k, qg[head, 0, slot]) * (SCALE * LOG2E) - st[head, slot, 0:1, :]
            s = jnp.where(row_id <= col_id, s, NEG) if slot == OWN else s + bias[1, slot]
            p = jnp.exp2(s)
            pk[:, span(slot)] = p.astype(jnp.bfloat16)
            yield
            dp = dot_nt(v, qg[head, 1, slot])
            dsk[:, span(slot)] = (p * (dp - st[head, slot, 1:2, :])).astype(jnp.bfloat16)
            yield
        ob[3, head] = dot_nn(pk[...], qg[head, 1].reshape(WIDE, HD)).astype(jnp.bfloat16)
        yield
        ob[2, head] = (dot_nn(dsk[...], qg[head, 0].reshape(WIDE, HD)) * SCALE).astype(jnp.bfloat16)

    def key_done(head):
        for c in stores(head, (2, 3)):
            c.start()

    def together(*parts):
        parts = list(parts)
        while parts:
            for part in tuple(parts):
                if next(part, True):
                    parts.remove(part)

    def query_side(head):
        query_waits(head)
        together(query_parts(head))
        query_done(head)

    def key_side(head):
        key_waits(head)
        together(key_parts(head))
        key_done(head)

    def both_sides(head, key_head):
        query_waits(head)
        key_waits(key_head)
        together(query_parts(head), key_parts(key_head))
        query_done(head)
        key_done(key_head)

    @pl.loop(0, H + KEY)
    def _(step):
        for stage, lag in (
            (own, 0),
            (relay(7, sends_7), ROW),
            (relay(5, sends_5), BACK),
            (relay(2, sends_2), NEAR),
            (relay(3, sends_3), FARTHER),
        ):

            @pl.when((step >= lag) & (step < H + lag))
            def _(stage=stage, lag=lag):
                stage(step - lag)

        @pl.when((step >= KEY) & (step < H + QUERY))
        def _():
            both_sides(step - QUERY, step - KEY)

        @pl.when((step >= QUERY) & (step < KEY))
        def _():
            query_side(step - QUERY)

        @pl.when(step >= H + QUERY)
        def _():
            key_side(step - KEY)

    for side in range(2):
        m = index[side]
        line, row = (m // 4) % 8, m // 32
        conds = (
            (m % 4 != 3) | (m >= 4),
            (m % 4 < 2) | (m >= 4),
            (line < 7) | (row >= 1),
            (m >= 4) & (m + 4 < NB),
            (m >= 8) & (m + 8 < NB),
            row != 3,
            row == 6,
            row < 4,
            (row >= 1) & (row < 7) & (row != 3),
        )
        for slot, cond in enumerate(conds):

            @pl.when(cond)
            def _(side=side, slot=slot):
                pltpu.make_async_remote_copy(
                    src_ref=bufs[side].at[:, :, OWN],
                    dst_ref=bufs[side].at[:, :, 0],
                    send_sem=send_sem.at[side, slot],
                    recv_sem=recv_sem.at[side, 0, 0],
                    device_id=place(me),
                    device_id_type=MESH,
                ).wait_send()

    for level in range(FAR):

        @pl.when(me >= 2**level)
        def _(level=level):
            pltpu.make_async_remote_copy(
                src_ref=st.at[:, OWN],
                dst_ref=st.at[:, level],
                send_sem=st_send.at[level],
                recv_sem=st_recv.at[level, 0],
                device_id=place(me - 2**level),
                device_id_type=MESH,
            ).wait_send()

    @pl.loop(0, H)
    def _(head):
        for c in stores(head, range(4)):
            c.wait()


def local(queries, keys, values, grad_out, level_mask):
    hbm = pl.BlockSpec(memory_space=pltpu.HBM)
    out = jax.ShapeDtypeStruct((BLK, H * HD), jnp.bfloat16)
    return tuple(
        pl.pallas_call(
            kernel,
            name="log_sparse",
            out_shape=(out, out, out, out),
            in_specs=[hbm] * 4 + [pl.BlockSpec(memory_space=pltpu.SMEM)],
            out_specs=(hbm,) * 4,
            scratch_shapes=[
                pltpu.VMEM((H, 2, SLOTS, BLK, HD), jnp.bfloat16),
                pltpu.VMEM((H, 2, SLOTS, BLK, HD), jnp.bfloat16),
                pltpu.VMEM((H, SLOTS, 8, BLK), jnp.float32),
                pltpu.VMEM((BLK, WIDE), jnp.float32),
                pltpu.VMEM((BLK, WIDE), jnp.bfloat16),
                pltpu.VMEM((BLK, WIDE), jnp.bfloat16),
                pltpu.VMEM((BLK, WIDE), jnp.bfloat16),
                pltpu.VMEM((BLK, WIDE), jnp.bfloat16),
                pltpu.VMEM((4, H, BLK, HD), jnp.bfloat16),
                pltpu.SMEM((2, FAR), jnp.float32),
                pltpu.SemaphoreType.DMA((4, H)),
                pltpu.SemaphoreType.DMA((2, FAR + 1)),
                pltpu.SemaphoreType.DMA((2, FAR, H)),
                pltpu.SemaphoreType.DMA((FAR,)),
                pltpu.SemaphoreType.DMA((FAR, H)),
                pltpu.SemaphoreType.DMA((4, H)),
            ],
            compiler_params=pltpu.CompilerParams(
                collective_id=0, has_side_effects=True, vmem_limit_bytes=63 << 20
            ),
        )(queries, keys, values, grad_out, level_mask)
    )


def solution(mesh):
    rows = P(("ctx", "head"), None)
    return jax.shard_map(
        local,
        mesh=mesh,
        in_specs=(rows, rows, rows, rows, P()),
        out_specs=(rows, rows, rows, rows),
        check_vma=False,
    )
```

```python
import jax
import jax.numpy as jnp
from jax import lax
from jax.experimental import pallas as pl
from jax.experimental.pallas import tpu as pltpu
from jax.sharding import PartitionSpec as P

HD = 128
BLK = 128
LEVELS = 9
NB = 256
H = 16
FAR = 8
OWN = FAR
SLOTS = FAR + 1
SECOND = FAR
WIDE = SLOTS * BLK
NEG = -1e30
SCALE = HD ** (-0.5)
LOG2E = 1.4426950408889634
MESH = pl.DeviceIdType.MESH

ROW = 1
BACK = 2
NEAR = 3
FARTHER = 4
QUERY = 5
KEY = 8


def dot_nt(a, b):
    return lax.dot_general(a, b, (((1,), (1,)), ((), ())), preferred_element_type=jnp.float32)


def dot_nn(a, b):
    return lax.dot_general(a, b, (((1,), (0,)), ((), ())), preferred_element_type=jnp.float32)


def place(block):
    return (block // 2, block % 2)


def kernel(
    q_hbm, k_hbm, v_hbm, g_hbm, lm_ref,
    o_hbm, dq_hbm, dk_hbm, dv_hbm,
    kv, qg, st, p_s, pb, dsb, pk, dsk, ob, bias,
    load_sem, send_sem, recv_sem, st_send, st_recv, out_sem,
):
    me = lax.axis_index("ctx") * 2 + lax.axis_index("head")
    bufs = (kv, qg)
    index = (me, NB - 1 - me)

    def real(side, m):
        return m if side == 0 else NB - 1 - m

    def copy(side, src, level, head, target):
        buf = bufs[side]
        slot = level
        level = 6 if level == SECOND else level
        return pltpu.make_async_remote_copy(
            src_ref=buf.at[head, :, src],
            dst_ref=buf.at[head, :, level],
            send_sem=send_sem.at[side, slot],
            recv_sem=recv_sem.at[side, level, head],
            device_id=place(real(side, target)),
            device_id_type=MESH,
        )

    def send(side, src, level, head, target, cond):
        @pl.when(cond)
        def _():
            copy(side, src, level, head, target).start()

    def wait_recv(side, level, head):
        @pl.when(index[side] >= 2**level)
        def _():
            copy(side, OWN, level, head, index[side]).wait_recv()

    def loads(head):
        cols = pl.ds(pl.multiple_of(head * HD, HD), HD)
        return [
            pltpu.make_async_copy(k_hbm.at[:, cols], kv.at[head, 0, OWN], load_sem.at[0, head]),
            pltpu.make_async_copy(v_hbm.at[:, cols], kv.at[head, 1, OWN], load_sem.at[1, head]),
            pltpu.make_async_copy(q_hbm.at[:, cols], qg.at[head, 0, OWN], load_sem.at[2, head]),
            pltpu.make_async_copy(g_hbm.at[:, cols], qg.at[head, 1, OWN], load_sem.at[3, head]),
        ]

    @pl.loop(0, H)
    def _(head):
        for c in loads(head):
            c.start()

    for level in range(FAR):
        d = 2**level
        bias[0, level] = jnp.where((lm_ref[level, me] == 1) & (me >= d), 0.0, NEG)
        later = jnp.minimum(me + d, NB - 1)
        bias[1, level] = jnp.where((lm_ref[level, later] == 1) & (me + d < NB), 0.0, NEG)

    barrier = pltpu.get_barrier_semaphore()
    part, line, row = me % 4, (me // 4) % 8, me // 32
    partners = [(3, part == 0), (-3, part == 3), (28, line == 0), (-28, line == 7)]
    partners += [(96, row == 4), (-96, row == 7), (96, row == 0), (-96, row == 3)]
    for level in range(FAR):
        d = 2**level
        partners += [(-d, me >= d), (d, me + d < NB)]
    count = 0
    for d, cond in partners:
        count = count + jnp.where(cond, 1, 0)

        @pl.when(cond)
        def _(d=d):
            pl.semaphore_signal(barrier, inc=1, device_id=place(me + d), device_id_type=MESH)

    pl.semaphore_wait(barrier, count)

    def sends_own(m):
        line, row = (m // 4) % 8, m // 32
        return [
            (2, m + 4, line < 7),
            (7, m + 128, row < 4),
            (5, m + 32, (row != 3) & (row < 7)),
            (0, m + 1, m % 4 != 3),
            (1, m + 2, m % 4 < 2),
        ]

    def sends_7(m):
        row = m // 32
        return [(5, m - 96, row == 7), (6, m - 64, row == 6)]

    def sends_5(m):
        line, row = (m // 4) % 8, m // 32
        return [(2, m - 28, (line == 7) & (row >= 1)), (SECOND, m + 32, (row >= 1) & (row < 7) & (row != 3))]

    def sends_2(m):
        return [
            (3, m + 4, (m >= 4) & (m + 4 < NB)),
            (0, m - 3, (m >= 4) & (m % 4 == 3)),
            (1, m - 2, (m >= 4) & (m % 4 >= 2)),
        ]

    def sends_3(m):
        return [(4, m + 8, (m >= 8) & (m + 8 < NB))]

    def own(head):
        for c in loads(head):
            c.wait()
        send_own(head)
        for side in range(2):
            for level in range(FAR):

                @pl.when(index[side] < 2**level)
                def _(side=side, level=level):
                    bufs[side][head, :, level] = jnp.zeros((2, BLK, HD), jnp.bfloat16)
                    if side == 1:
                        st[head, level] = jnp.zeros((8, BLK), jnp.float32)

    def send_own(head):
        for i in range(5):
            for side in range(2):
                level, target, cond = sends_own(index[side])[i]
                send(side, OWN, level, head, target, cond)

    def relay(slot, sends):
        def stage(head):
            for side in range(2):
                wait_recv(side, slot, head)
                for level, target, cond in sends(index[side]):
                    send(side, slot, level, head, target, cond)

        return stage

    def stat_copy(level, head):
        return pltpu.make_async_remote_copy(
            src_ref=st.at[head, OWN],
            dst_ref=st.at[head, level],
            send_sem=st_send.at[level],
            recv_sem=st_recv.at[level, head],
            device_id=place(me - 2**level),
            device_id_type=MESH,
        )

    def stores(head, which):
        cols = pl.ds(pl.multiple_of(head * HD, HD), HD)
        return [
            pltpu.make_async_copy(ob.at[i, head], (o_hbm, dq_hbm, dk_hbm, dv_hbm)[i].at[:, cols], out_sem.at[i, head])
            for i in which
        ]

    row_id = lax.broadcasted_iota(jnp.int32, (BLK, BLK), 0)
    col_id = lax.broadcasted_iota(jnp.int32, (BLK, BLK), 1)

    def span(slot):
        return pl.ds(slot * BLK, BLK)

    def query_waits(head):
        for level in (0, 1, 6, 4):
            wait_recv(0, level, head)

    def key_waits(head):
        for level in (0, 1, 6, 4):
            wait_recv(1, level, head)
        for level in range(FAR):

            @pl.when(me + 2**level < NB)
            def _(level=level):
                stat_copy(level, head).wait_recv()

    def query_parts(head):
        q = qg[head, 0, OWN]
        g = qg[head, 1, OWN]
        top = None
        for slot in range(SLOTS):
            s = dot_nt(q, kv[head, 0, slot]) * (SCALE * LOG2E)
            s = jnp.where(row_id >= col_id, s, NEG) if slot == OWN else s + bias[0, slot]
            p_s[:, span(slot)] = s
            top = s if top is None else jnp.maximum(top, s)
            yield
        top = jnp.max(top, axis=1, keepdims=True)
        yield
        total = None
        for slot in range(SLOTS):
            p = jnp.exp2(p_s[:, span(slot)] - top)
            p_s[:, span(slot)] = p
            pb[:, span(slot)] = p.astype(jnp.bfloat16)
            total = p if total is None else total + p
            yield
        total = jnp.sum(total, axis=1, keepdims=True)
        inverse = 1.0 / total
        o = dot_nn(pb[...], kv[head, 1].reshape(WIDE, HD)) * inverse
        o = o.astype(jnp.bfloat16)
        ob[0, head] = o
        delta = jnp.sum(g.astype(jnp.float32) * o.astype(jnp.float32), axis=1, keepdims=True)
        lse = top + jnp.log2(total)
        yield
        for slot in range(SLOTS):
            dp = dot_nt(g, kv[head, 1, slot])
            dsb[:, span(slot)] = (p_s[:, span(slot)] * (dp - delta)).astype(jnp.bfloat16)
            yield
        dq = dot_nn(dsb[...], kv[head, 0].reshape(WIDE, HD)) * (inverse * SCALE)
        ob[1, head] = dq.astype(jnp.bfloat16)
        st[head, OWN] = jnp.where(col_id == 0, lse, delta).T[:8]

    def query_done(head):
        for level in range(FAR):

            @pl.when(me >= 2**level)
            def _(level=level):
                stat_copy(level, head).start()

        for c in stores(head, (0, 1)):
            c.start()

    def key_parts(head):
        k = kv[head, 0, OWN]
        v = kv[head, 1, OWN]
        for slot in range(SLOTS):
            s = dot_nt(k, qg[head, 0, slot]) * (SCALE * LOG2E) - st[head, slot, 0:1, :]
            s = jnp.where(row_id <= col_id, s, NEG) if slot == OWN else s + bias[1, slot]
            p = jnp.exp2(s)
            pk[:, span(slot)] = p.astype(jnp.bfloat16)
            yield
            dp = dot_nt(v, qg[head, 1, slot])
            dsk[:, span(slot)] = (p * (dp - st[head, slot, 1:2, :])).astype(jnp.bfloat16)
            yield
        ob[3, head] = dot_nn(pk[...], qg[head, 1].reshape(WIDE, HD)).astype(jnp.bfloat16)
        yield
        ob[2, head] = (dot_nn(dsk[...], qg[head, 0].reshape(WIDE, HD)) * SCALE).astype(jnp.bfloat16)

    def key_done(head):
        for c in stores(head, (2, 3)):
            c.start()

    def together(*parts):
        parts = list(parts)
        while parts:
            for part in tuple(parts):
                if next(part, True):
                    parts.remove(part)

    def query_side(head):
        query_waits(head)
        together(query_parts(head))
        query_done(head)

    def key_side(head):
        key_waits(head)
        together(key_parts(head))
        key_done(head)

    def both_sides(head, key_head):
        query_waits(head)
        key_waits(key_head)
        together(query_parts(head), key_parts(key_head))
        query_done(head)
        key_done(key_head)

    @pl.loop(0, H + KEY)
    def _(step):
        for stage, lag in (
            (own, 0),
            (relay(7, sends_7), ROW),
            (relay(5, sends_5), BACK),
            (relay(2, sends_2), NEAR),
            (relay(3, sends_3), FARTHER),
        ):

            @pl.when((step >= lag) & (step < H + lag))
            def _(stage=stage, lag=lag):
                stage(step - lag)

        @pl.when((step >= KEY) & (step < H + QUERY))
        def _():
            both_sides(step - QUERY, step - KEY)

        @pl.when((step >= QUERY) & (step < KEY))
        def _():
            query_side(step - QUERY)

        @pl.when(step >= H + QUERY)
        def _():
            key_side(step - KEY)

    for side in range(2):
        m = index[side]
        line, row = (m // 4) % 8, m // 32
        conds = (
            (m % 4 != 3) | (m >= 4),
            (m % 4 < 2) | (m >= 4),
            (line < 7) | (row >= 1),
            (m >= 4) & (m + 4 < NB),
            (m >= 8) & (m + 8 < NB),
            row != 3,
            row == 6,
            row < 4,
            (row >= 1) & (row < 7) & (row != 3),
        )
        for slot, cond in enumerate(conds):

            @pl.when(cond)
            def _(side=side, slot=slot):
                pltpu.make_async_remote_copy(
                    src_ref=bufs[side].at[:, :, OWN],
                    dst_ref=bufs[side].at[:, :, 0],
                    send_sem=send_sem.at[side, slot],
                    recv_sem=recv_sem.at[side, 0, 0],
                    device_id=place(me),
                    device_id_type=MESH,
                ).wait_send()

    for level in range(FAR):

        @pl.when(me >= 2**level)
        def _(level=level):
            pltpu.make_async_remote_copy(
                src_ref=st.at[:, OWN],
                dst_ref=st.at[:, level],
                send_sem=st_send.at[level],
                recv_sem=st_recv.at[level, 0],
                device_id=place(me - 2**level),
                device_id_type=MESH,
            ).wait_send()

    @pl.loop(0, H)
    def _(head):
        for c in stores(head, range(4)):
            c.wait()


def local(queries, keys, values, grad_out, level_mask):
    hbm = pl.BlockSpec(memory_space=pltpu.HBM)
    out = jax.ShapeDtypeStruct((BLK, H * HD), jnp.bfloat16)
    return tuple(
        pl.pallas_call(
            kernel,
            name="log_sparse",
            out_shape=(out, out, out, out),
            in_specs=[hbm] * 4 + [pl.BlockSpec(memory_space=pltpu.SMEM)],
            out_specs=(hbm,) * 4,
            scratch_shapes=[
                pltpu.VMEM((H, 2, SLOTS, BLK, HD), jnp.bfloat16),
                pltpu.VMEM((H, 2, SLOTS, BLK, HD), jnp.bfloat16),
                pltpu.VMEM((H, SLOTS, 8, BLK), jnp.float32),
                pltpu.VMEM((BLK, WIDE), jnp.float32),
                pltpu.VMEM((BLK, WIDE), jnp.bfloat16),
                pltpu.VMEM((BLK, WIDE), jnp.bfloat16),
                pltpu.VMEM((BLK, WIDE), jnp.bfloat16),
                pltpu.VMEM((BLK, WIDE), jnp.bfloat16),
                pltpu.VMEM((4, H, BLK, HD), jnp.bfloat16),
                pltpu.SMEM((2, FAR), jnp.float32),
                pltpu.SemaphoreType.DMA((4, H)),
                pltpu.SemaphoreType.DMA((2, FAR + 1)),
                pltpu.SemaphoreType.DMA((2, FAR, H)),
                pltpu.SemaphoreType.DMA((FAR,)),
                pltpu.SemaphoreType.DMA((FAR, H)),
                pltpu.SemaphoreType.DMA((4, H)),
            ],
            compiler_params=pltpu.CompilerParams(
                collective_id=0, has_side_effects=True, vmem_limit_bytes=63 << 20
            ),
        )(queries, keys, values, grad_out, level_mask.T)
    )


def solution(mesh):
    rows = P(("ctx", "head"), None)
    return jax.shard_map(
        local,
        mesh=mesh,
        in_specs=(rows, rows, rows, rows, P()),
        out_specs=(rows, rows, rows, rows),
        check_vma=False,
    )
```

```python
import jax
import jax.numpy as jnp
from jax import lax
from jax.experimental import pallas as pl
from jax.experimental.pallas import tpu as pltpu
from jax.sharding import PartitionSpec as P

HD = 128
BLK = 128
LEVELS = 9
NB = 256
H = 16
FAR = 8
OWN = FAR
SLOTS = FAR + 1
SECOND = FAR
WIDE = SLOTS * BLK
NEG = -1e30
SCALE = HD ** (-0.5)
LOG2E = 1.4426950408889634
MESH = pl.DeviceIdType.MESH

ROW = 1
BACK = 2
NEAR = 3
FARTHER = 4
QUERY = 5
KEY = 8


def dot_nt(a, b):
    return lax.dot_general(a, b, (((1,), (1,)), ((), ())), preferred_element_type=jnp.float32)


def dot_nn(a, b):
    return lax.dot_general(a, b, (((1,), (0,)), ((), ())), preferred_element_type=jnp.float32)


def place(block):
    return (block // 2, block % 2)


def kernel(
    q_hbm, k_hbm, v_hbm, g_hbm, lm_ref,
    o_hbm, dq_hbm, dk_hbm, dv_hbm,
    kv, qg, st, p_s, pb, dsb, pk, dsk, ob, bias,
    load_sem, send_sem, recv_sem, st_send, st_recv, out_sem,
):
    me = lax.axis_index("ctx") * 2 + lax.axis_index("head")
    bufs = (kv, qg)
    index = (me, NB - 1 - me)

    def real(side, m):
        return m if side == 0 else NB - 1 - m

    def copy(side, src, level, head, target):
        buf = bufs[side]
        slot = level
        level = 6 if level == SECOND else level
        return pltpu.make_async_remote_copy(
            src_ref=buf.at[head, :, src],
            dst_ref=buf.at[head, :, level],
            send_sem=send_sem.at[side, slot],
            recv_sem=recv_sem.at[side, level, head],
            device_id=place(real(side, target)),
            device_id_type=MESH,
        )

    def send(side, src, level, head, target, cond):
        @pl.when(cond)
        def _():
            copy(side, src, level, head, target).start()

    def wait_recv(side, level, head):
        @pl.when(index[side] >= 2**level)
        def _():
            copy(side, OWN, level, head, index[side]).wait_recv()

    def loads(head):
        cols = pl.ds(pl.multiple_of(head * HD, HD), HD)
        return [
            pltpu.make_async_copy(k_hbm.at[:, cols], kv.at[head, 0, OWN], load_sem.at[0, head]),
            pltpu.make_async_copy(v_hbm.at[:, cols], kv.at[head, 1, OWN], load_sem.at[1, head]),
            pltpu.make_async_copy(q_hbm.at[:, cols], qg.at[head, 0, OWN], load_sem.at[2, head]),
            pltpu.make_async_copy(g_hbm.at[:, cols], qg.at[head, 1, OWN], load_sem.at[3, head]),
        ]

    @pl.loop(0, H)
    def _(head):
        for c in loads(head):
            c.start()

    for level in range(FAR):
        d = 2**level
        bias[0, level] = jnp.where((lm_ref[level, me] == 1) & (me >= d), 0.0, NEG)
        later = jnp.minimum(me + d, NB - 1)
        bias[1, level] = jnp.where((lm_ref[level, later] == 1) & (me + d < NB), 0.0, NEG)

    barrier = pltpu.get_barrier_semaphore()
    part, line, row = me % 4, (me // 4) % 8, me // 32
    partners = [(3, part == 0), (-3, part == 3), (28, line == 0), (-28, line == 7)]
    partners += [(96, row == 4), (-96, row == 7), (96, row == 0), (-96, row == 3)]
    for level in range(FAR):
        d = 2**level
        partners += [(-d, me >= d), (d, me + d < NB)]
    count = 0
    for d, cond in partners:
        count = count + jnp.where(cond, 1, 0)

        @pl.when(cond)
        def _(d=d):
            pl.semaphore_signal(barrier, inc=1, device_id=place(me + d), device_id_type=MESH)

    pl.semaphore_wait(barrier, count)

    def sends_own(m):
        line, row = (m // 4) % 8, m // 32
        return [
            (2, m + 4, line < 7),
            (7, m + 128, row < 4),
            (5, m + 32, (row != 3) & (row < 7)),
        ]

    def sends_7(m):
        row = m // 32
        return [(5, m - 96, row == 7), (6, m - 64, row == 6)]

    def sends_5(m):
        line, row = (m // 4) % 8, m // 32
        return [(2, m - 28, (line == 7) & (row >= 1)), (SECOND, m + 32, (row >= 1) & (row < 7) & (row != 3))]

    def sends_2(m):
        return [
            (3, m + 4, (m >= 4) & (m + 4 < NB)),
            (0, m - 3, (m >= 4) & (m % 4 == 3)),
            (1, m - 2, (m >= 4) & (m % 4 >= 2)),
        ]

    def sends_3(m):
        return [(4, m + 8, (m >= 8) & (m + 8 < NB))]

    def own(head):
        for c in loads(head):
            c.wait()
        send_own(head)
        for side in range(2):
            for level in range(FAR):

                @pl.when(index[side] < 2**level)
                def _(side=side, level=level):
                    bufs[side][head, :, level] = jnp.zeros((2, BLK, HD), jnp.bfloat16)
                    if side == 1:
                        st[head, level] = jnp.zeros((8, BLK), jnp.float32)

    def send_own(head):
        for i in range(3):
            for side in range(2):
                level, target, cond = sends_own(index[side])[i]
                send(side, OWN, level, head, target, cond)

    def relay(slot, sends):
        def stage(head):
            for side in range(2):
                wait_recv(side, slot, head)
                for level, target, cond in sends(index[side]):
                    send(side, slot, level, head, target, cond)
                if slot == 2:
                    m = index[side]
                    send(side, OWN, 0, head, m + 1, m % 4 != 3)
                    send(side, OWN, 1, head, m + 2, m % 4 < 2)

        return stage

    def stat_copy(level, head):
        return pltpu.make_async_remote_copy(
            src_ref=st.at[head, OWN],
            dst_ref=st.at[head, level],
            send_sem=st_send.at[level],
            recv_sem=st_recv.at[level, head],
            device_id=place(me - 2**level),
            device_id_type=MESH,
        )

    def stores(head, which):
        cols = pl.ds(pl.multiple_of(head * HD, HD), HD)
        return [
            pltpu.make_async_copy(ob.at[i, head], (o_hbm, dq_hbm, dk_hbm, dv_hbm)[i].at[:, cols], out_sem.at[i, head])
            for i in which
        ]

    row_id = lax.broadcasted_iota(jnp.int32, (BLK, BLK), 0)
    col_id = lax.broadcasted_iota(jnp.int32, (BLK, BLK), 1)

    def span(slot):
        return pl.ds(slot * BLK, BLK)

    def query_waits(head):
        for level in (0, 1, 6, 4):
            wait_recv(0, level, head)

    def key_waits(head):
        for level in (0, 1, 6, 4):
            wait_recv(1, level, head)
        for level in range(FAR):

            @pl.when(me + 2**level < NB)
            def _(level=level):
                stat_copy(level, head).wait_recv()

    def query_parts(head):
        q = qg[head, 0, OWN]
        g = qg[head, 1, OWN]
        top = None
        for slot in range(SLOTS):
            s = dot_nt(q, kv[head, 0, slot]) * (SCALE * LOG2E)
            s = jnp.where(row_id >= col_id, s, NEG) if slot == OWN else s + bias[0, slot]
            p_s[:, span(slot)] = s
            top = s if top is None else jnp.maximum(top, s)
            yield
        top = jnp.max(top, axis=1, keepdims=True)
        yield
        total = None
        for slot in range(SLOTS):
            p = jnp.exp2(p_s[:, span(slot)] - top)
            p_s[:, span(slot)] = p
            pb[:, span(slot)] = p.astype(jnp.bfloat16)
            total = p if total is None else total + p
            yield
        total = jnp.sum(total, axis=1, keepdims=True)
        inverse = 1.0 / total
        o = dot_nn(pb[...], kv[head, 1].reshape(WIDE, HD)) * inverse
        o = o.astype(jnp.bfloat16)
        ob[0, head] = o
        delta = jnp.sum(g.astype(jnp.float32) * o.astype(jnp.float32), axis=1, keepdims=True)
        lse = top + jnp.log2(total)
        yield
        for slot in range(SLOTS):
            dp = dot_nt(g, kv[head, 1, slot])
            dsb[:, span(slot)] = (p_s[:, span(slot)] * (dp - delta)).astype(jnp.bfloat16)
            yield
        dq = dot_nn(dsb[...], kv[head, 0].reshape(WIDE, HD)) * (inverse * SCALE)
        ob[1, head] = dq.astype(jnp.bfloat16)
        st[head, OWN] = jnp.where(col_id == 0, lse, delta).T[:8]

    def query_done(head):
        for level in range(FAR):

            @pl.when(me >= 2**level)
            def _(level=level):
                stat_copy(level, head).start()

        for c in stores(head, (0, 1)):
            c.start()

    def key_parts(head):
        k = kv[head, 0, OWN]
        v = kv[head, 1, OWN]
        for slot in range(SLOTS):
            s = dot_nt(k, qg[head, 0, slot]) * (SCALE * LOG2E) - st[head, slot, 0:1, :]
            s = jnp.where(row_id <= col_id, s, NEG) if slot == OWN else s + bias[1, slot]
            p = jnp.exp2(s)
            pk[:, span(slot)] = p.astype(jnp.bfloat16)
            yield
            dp = dot_nt(v, qg[head, 1, slot])
            dsk[:, span(slot)] = (p * (dp - st[head, slot, 1:2, :])).astype(jnp.bfloat16)
            yield
        ob[3, head] = dot_nn(pk[...], qg[head, 1].reshape(WIDE, HD)).astype(jnp.bfloat16)
        yield
        ob[2, head] = (dot_nn(dsk[...], qg[head, 0].reshape(WIDE, HD)) * SCALE).astype(jnp.bfloat16)

    def key_done(head):
        for c in stores(head, (2, 3)):
            c.start()

    def together(*parts):
        parts = list(parts)
        while parts:
            for part in tuple(parts):
                if next(part, True):
                    parts.remove(part)

    def query_side(head):
        query_waits(head)
        together(query_parts(head))
        query_done(head)

    def key_side(head):
        key_waits(head)
        together(key_parts(head))
        key_done(head)

    def both_sides(head, key_head):
        query_waits(head)
        key_waits(key_head)
        together(query_parts(head), key_parts(key_head))
        query_done(head)
        key_done(key_head)

    @pl.loop(0, H + KEY)
    def _(step):
        for stage, lag in (
            (own, 0),
            (relay(7, sends_7), ROW),
            (relay(5, sends_5), BACK),
            (relay(2, sends_2), NEAR),
            (relay(3, sends_3), FARTHER),
        ):

            @pl.when((step >= lag) & (step < H + lag))
            def _(stage=stage, lag=lag):
                stage(step - lag)

        @pl.when((step >= KEY) & (step < H + QUERY))
        def _():
            both_sides(step - QUERY, step - KEY)

        @pl.when((step >= QUERY) & (step < KEY))
        def _():
            query_side(step - QUERY)

        @pl.when(step >= H + QUERY)
        def _():
            key_side(step - KEY)

    for side in range(2):
        m = index[side]
        line, row = (m // 4) % 8, m // 32
        conds = (
            (m % 4 != 3) | (m >= 4),
            (m % 4 < 2) | (m >= 4),
            (line < 7) | (row >= 1),
            (m >= 4) & (m + 4 < NB),
            (m >= 8) & (m + 8 < NB),
            row != 3,
            row == 6,
            row < 4,
            (row >= 1) & (row < 7) & (row != 3),
        )
        for slot, cond in enumerate(conds):

            @pl.when(cond)
            def _(side=side, slot=slot):
                pltpu.make_async_remote_copy(
                    src_ref=bufs[side].at[:, :, OWN],
                    dst_ref=bufs[side].at[:, :, 0],
                    send_sem=send_sem.at[side, slot],
                    recv_sem=recv_sem.at[side, 0, 0],
                    device_id=place(me),
                    device_id_type=MESH,
                ).wait_send()

    for level in range(FAR):

        @pl.when(me >= 2**level)
        def _(level=level):
            pltpu.make_async_remote_copy(
                src_ref=st.at[:, OWN],
                dst_ref=st.at[:, level],
                send_sem=st_send.at[level],
                recv_sem=st_recv.at[level, 0],
                device_id=place(me - 2**level),
                device_id_type=MESH,
            ).wait_send()

    @pl.loop(0, H)
    def _(head):
        for c in stores(head, range(4)):
            c.wait()


def local(queries, keys, values, grad_out, level_mask):
    hbm = pl.BlockSpec(memory_space=pltpu.HBM)
    out = jax.ShapeDtypeStruct((BLK, H * HD), jnp.bfloat16)
    return tuple(
        pl.pallas_call(
            kernel,
            name="log_sparse",
            out_shape=(out, out, out, out),
            in_specs=[hbm] * 4 + [pl.BlockSpec(memory_space=pltpu.SMEM)],
            out_specs=(hbm,) * 4,
            scratch_shapes=[
                pltpu.VMEM((H, 2, SLOTS, BLK, HD), jnp.bfloat16),
                pltpu.VMEM((H, 2, SLOTS, BLK, HD), jnp.bfloat16),
                pltpu.VMEM((H, SLOTS, 8, BLK), jnp.float32),
                pltpu.VMEM((BLK, WIDE), jnp.float32),
                pltpu.VMEM((BLK, WIDE), jnp.bfloat16),
                pltpu.VMEM((BLK, WIDE), jnp.bfloat16),
                pltpu.VMEM((BLK, WIDE), jnp.bfloat16),
                pltpu.VMEM((BLK, WIDE), jnp.bfloat16),
                pltpu.VMEM((4, H, BLK, HD), jnp.bfloat16),
                pltpu.SMEM((2, FAR), jnp.float32),
                pltpu.SemaphoreType.DMA((4, H)),
                pltpu.SemaphoreType.DMA((2, FAR + 1)),
                pltpu.SemaphoreType.DMA((2, FAR, H)),
                pltpu.SemaphoreType.DMA((FAR,)),
                pltpu.SemaphoreType.DMA((FAR, H)),
                pltpu.SemaphoreType.DMA((4, H)),
            ],
            compiler_params=pltpu.CompilerParams(
                collective_id=0, has_side_effects=True, vmem_limit_bytes=63 << 20
            ),
        )(queries, keys, values, grad_out, level_mask.T)
    )


def solution(mesh):
    rows = P(("ctx", "head"), None)
    return jax.shard_map(
        local,
        mesh=mesh,
        in_specs=(rows, rows, rows, rows, P()),
        out_specs=(rows, rows, rows, rows),
        check_vma=False,
    )
```
